32 devices in a mesh: tgt: 8 (over z, x), src: 4 (over y, core).
Axes of the slice: x: 2, y: 2, z: 4, core: 2. Of those that a mesh axis runs over, the one named last changes fastest.
Arguments:
- target_points: float32 [3, 8, 4096], P(None, None, 'src'), may hold values from 0 to 1
- source_points: float32 [3, 4096], P(None, 'tgt'), may hold values from 0 to 1
- charges: float32 [4096], P('tgt'), may hold values from 0.1 to 1
- sketch: bfloat16 [128, 4096], P(None, 'tgt'), may hold values from -0.09375 to 0.09375
- far_mask: int32 [8, 32], replicated, may hold values 0 or 1
Outputs:
- range_basis: bfloat16 [8, 4096, 128], P('tgt', 'src')
- far_factor: bfloat16 [8, 128, 4096], P('tgt', None, 'src')
The draws below stay inside these ranges and needn't reach their ends.
All inputs are finite; a program needn't handle non-finite values.
Results may differ from the reference program's by a relative error of at most 0.02.
Values may be sent and summed in bfloat16 or wider, within the bound.
A program may use at most 128 MiB of HBM per device.

```python
import math
import jax
import jax.numpy as jnp
from jax import lax

MT = 4096
RANK = 128
SRC_DEV = 512
CLUSTER_SIZE = 128
BR = 8
SOURCES = 4096
CLUSTERS = 32
N_TGT = 8
N_SRC = 4


def set_ends(drawn, key, low, high):
    longest = drawn.shape.index(max(drawn.shape))
    spots = []
    for shift in (0, 1):
        where = [jax.random.randint(jax.random.fold_in(key, axis), (), 0, length) for axis, length in enumerate(drawn.shape)]
        where[longest] = (where[longest] + shift) % drawn.shape[longest]
        spots.append(tuple(where))
    return drawn.at[spots[0]].set(low).at[spots[1]].set(high)


def level_of(own_key, shape, pieces, smallest, top_value):
    level = 1.0
    for position, blocks in pieces:
        steps = jax.random.uniform(jax.random.fold_in(jax.random.fold_in(own_key, 6), position), (blocks,), jnp.float32, smallest / len(pieces), top_value / len(pieces))
        level = level * jnp.repeat(jnp.exp(steps), shape[position] // blocks).reshape((-1,) + (1,) * (len(shape) - 1 - position))
    return level


def scatter_about(key, shape, scale, limit, split=(), held_as=jnp.bfloat16):
    values = scale * jax.random.normal(key, shape, jnp.float32)
    if split:
        values = values * level_of(key, shape, split, -0.22, 0.18)
    return jnp.clip(values, -limit, limit).astype(held_as)


def setup_inputs(seed: int = 0) -> dict:
    splits = jax.random.split(jax.random.key(seed), 6)
    return {
        "target_points": jnp.clip(1.0 * jax.random.uniform(splits[0], (3, BR, MT), jnp.float32) ** level_of(splits[0], (3, BR, MT), ((2, 4),), -0.2, 0.2), 0.0, 1.0),
        "source_points": jnp.clip(1.0 * jax.random.uniform(splits[1], (3, SOURCES), jnp.float32) ** level_of(splits[1], (3, SOURCES), ((1, 8),), -0.2, 0.2), 0.0, 1.0),
        "charges": jnp.clip(jnp.exp(math.log(1.0) - 2.3025851 * jax.random.uniform(splits[2], (SOURCES,), jnp.float32) ** level_of(splits[2], (SOURCES,), ((0, 8),), -0.2, 0.2)), 0.1, 1.0),
        "sketch": scatter_about(splits[3], (RANK, SOURCES), SOURCES ** -0.5, 0.09375, ((1, 8),)),
        "far_mask": set_ends((jax.random.randint(splits[4], (BR, CLUSTERS), 0, 4) < 3).astype(jnp.int32), jax.random.fold_in(splits[4], 1), 0, 1),
    }


SOFTENING = 0.0004
SHIFT_SCALE = 0.05

def kernel_tile(targets, sources, weight):
    delta_x = targets[0][:, None] - sources[0][None, :]
    delta_y = targets[1][:, None] - sources[1][None, :]
    delta_z = targets[2][:, None] - sources[2][None, :]
    distance2 = delta_x * delta_x + delta_y * delta_y + delta_z * delta_z + SOFTENING
    return (weight[None, :] / jnp.sqrt(distance2)).astype(jnp.bfloat16)

def reference(target_points, source_points, charges, sketch, far_mask):
    rows_dev = MT // N_SRC
    weights_all = jnp.repeat(far_mask, CLUSTER_SIZE, axis=1).astype(jnp.float32) * charges[None, :]
    source_blocks = jnp.transpose(source_points.reshape(3, N_TGT, SRC_DEV), (1, 0, 2))
    sketch_blocks = jnp.transpose(sketch.reshape(RANK, N_TGT, SRC_DEV), (1, 0, 2))

    def one_row(row_inputs):
        targets, weight_row = row_inputs
        weight_blocks = weight_row.reshape(N_TGT, SRC_DEV)

        def add_block(running, block_inputs):
            points, columns, weight = block_inputs
            kernel_block = kernel_tile(targets, points, weight)
            product = lax.dot_general(kernel_block.astype(jnp.float32), columns.astype(jnp.float32), (((1,), (1,)), ((), ())), preferred_element_type=jnp.float32)
            return (running + product, None)
        sketched, _ = lax.scan(add_block, jnp.zeros((MT, RANK), jnp.float32), (source_blocks, sketch_blocks, weight_blocks))
        gram_matrix = jnp.dot(sketched.T, sketched, precision=lax.Precision.HIGHEST)
        diag_shift = SHIFT_SCALE * jnp.trace(gram_matrix) / RANK
        lower_factor = jnp.linalg.cholesky(gram_matrix + diag_shift * jnp.eye(RANK, dtype=jnp.float32))
        solved = lax.linalg.triangular_solve(lower_factor, sketched.T, left_side=True, lower=True)
        range_basis = (math.sqrt(MT) * solved.T).astype(jnp.bfloat16)
        basis_slices = range_basis.reshape(N_SRC, rows_dev, RANK).astype(jnp.float32)

        def project(block_inputs):
            points, weight = block_inputs
            kernel_block = kernel_tile(targets, points, weight).reshape(N_SRC, rows_dev, SRC_DEV).astype(jnp.float32)
            slice_parts = jnp.einsum('smr,smn->srn', basis_slices, kernel_block, precision=lax.Precision.HIGHEST) * (1.0 / MT)
            rounded = lax.optimization_barrier(slice_parts.astype(jnp.bfloat16))
            return lax.optimization_barrier(jnp.sum(rounded.astype(jnp.float32), axis=0)).astype(jnp.bfloat16)
        factor = lax.map(project, (source_blocks, weight_blocks))
        factor = jnp.transpose(factor, (1, 0, 2)).reshape(RANK, SOURCES)
        return (range_basis, factor)
    range_basis, far_factor = lax.map(one_row, (jnp.moveaxis(target_points, 1, 0), weights_all))
    return (range_basis, far_factor)
```

```python
import functools
import math

import jax
import jax.numpy as jnp
from jax import lax
from jax.experimental import pallas as pl
from jax.experimental.pallas import tpu as pltpu
from jax.sharding import PartitionSpec as P

SOFTENING = 0.0004
SHIFT_SCALE = 0.05
MESH = pl.DeviceIdType.MESH
HIGHEST = lax.Precision.HIGHEST
F32 = jnp.float32
BF16 = jnp.bfloat16
VMEM_LIMIT = 56 << 20


def remote(src, dst, send_sem, recv_sem, device):
    return pltpu.make_async_remote_copy(
        src_ref=src, dst_ref=dst, send_sem=send_sem, recv_sem=recv_sem,
        device_id=device, device_id_type=MESH,
    )


def sketch_kernel(
    n_t, n_s, cluster, targets_ref, points_ref, charges_ref, sketch_ref, mask_ref,
    kernel_out, sketched_ref, gram_ref,
    packed, columns, kernel_all, target_cols, grams,
    pk_send, pk_recv, sk_send, sk_recv, mate_send, mate_recv, g_send, g_recv, out_sem,
):
    t = lax.axis_index("tgt")
    s = lax.axis_index("src")
    core = s % 2
    mate = s + 1 - 2 * core
    rank, width = sketch_ref.shape
    rows = targets_ref.shape[2]
    half = rank // 2

    barrier = pltpu.get_barrier_semaphore()
    for d in range(1, n_t):
        pl.semaphore_signal(barrier, inc=1, device_id=((t + d) % n_t, s), device_id_type=MESH)
    for d in range(1, n_s):
        pl.semaphore_signal(barrier, inc=1, device_id=(t, (s + d) % n_s), device_id_type=MESH)

    packed[t, 0:3, :] = points_ref[...]
    packed[t, 3:4, :] = charges_ref[...]
    columns[t] = sketch_ref[...]
    pl.semaphore_wait(barrier, n_t + n_s - 2)

    def halves(owner, which):
        return columns.at[owner, pl.ds(pl.multiple_of(which * half, half), half)]

    def packed_copy(d):
        return remote(packed.at[t], packed.at[t], pk_send.at[d], pk_recv.at[t], ((t + d) % n_t, s))

    def half_copy(d):
        return remote(halves(t, core), halves(t, core), sk_send.at[d], sk_recv.at[t], ((t + d) % n_t, s))

    def mate_copy(owner):
        return remote(halves(owner, core), halves(owner, core), mate_send.at[owner], mate_recv.at[owner], (t, mate))

    def out_copy(owner):
        return pltpu.make_async_copy(kernel_all.at[owner], kernel_out.at[owner], out_sem.at[owner])

    for d in range(1, n_t):
        packed_copy(d).start()
    for d in range(1, n_t):
        half_copy(d).start()

    lanes = 128
    stacked = jnp.concatenate(
        [targets_ref[0, pl.ds(t, 1), :], targets_ref[1, pl.ds(t, 1), :], targets_ref[2, pl.ds(t, 1), :],
         jnp.zeros((5, rows), F32)], axis=0)
    for first in range(0, rows, 128):
        block = jnp.concatenate([stacked[:, first:first + 128], jnp.zeros((120, 128), F32)], axis=0).T
        for axis in range(3):
            target_cols[axis, first:first + 128, :] = jnp.broadcast_to(block[:, axis:axis + 1], (128, lanes))
    sketched_ref[...] = jnp.zeros_like(sketched_ref)

    chunk = 256
    sub = 64

    def sweep(owner, previous):
        sx, sy, sz = packed[owner, 0:1, :], packed[owner, 1:2, :], packed[owner, 2:3, :]
        charge = packed[owner, 3:4, :]
        weights = []
        for piece in range(width // lanes):
            near = mask_ref[t, owner * (width // cluster) + piece * lanes // cluster]
            weights.append(charge[:, piece * lanes:(piece + 1) * lanes] * near.astype(F32))

        def step(index, carry):
            base = pl.multiple_of(index * chunk, chunk)
            for inner in range(chunk // sub):
                at = pl.ds(base + inner * sub, sub)
                tx, ty, tz = target_cols[0, at, :], target_cols[1, at, :], target_cols[2, at, :]
                for piece in range(width // lanes):
                    cut = slice(piece * lanes, (piece + 1) * lanes)
                    dx = tx - sx[:, cut]
                    dy = ty - sy[:, cut]
                    dz = tz - sz[:, cut]
                    distance2 = dx * dx + dy * dy + dz * dz + SOFTENING
                    kernel_all[owner, at, cut] = (weights[piece] * lax.rsqrt(distance2)).astype(BF16)
            if previous is not None:
                at = pl.ds(base, chunk)
                sketched_ref[at, :] += lax.dot_general(
                    kernel_all[previous, at, :], columns[previous], (((1,), (1,)), ((), ())),
                    preferred_element_type=F32)
            return carry

        lax.fori_loop(0, rows // chunk, step, 0)

    sweep(t, None)
    out_copy(t).start()

    def visit(d, carry):
        owner = (t + n_t - d) % n_t
        previous = (t + n_t - d + 1) % n_t
        pltpu.make_async_copy(packed.at[owner], packed.at[owner], pk_recv.at[owner]).wait()

        @pl.when(d >= 2)
        def _():
            pltpu.make_async_copy(halves(previous, 1 - core), halves(previous, 1 - core), mate_recv.at[previous]).wait()

        sweep(owner, previous)
        out_copy(owner).start()
        pltpu.make_async_copy(halves(owner, core), halves(owner, core), sk_recv.at[owner]).wait()
        mate_copy(owner).start()
        return carry

    lax.fori_loop(1, n_t, visit, 0)
    last = (t + 1) % n_t
    pltpu.make_async_copy(halves(last, 1 - core), halves(last, 1 - core), mate_recv.at[last]).wait()

    def finish(index, carry):
        at = pl.ds(pl.multiple_of(index * chunk, chunk), chunk)
        sketched_ref[at, :] += lax.dot_general(
            kernel_all[last, at, :], columns[last], (((1,), (1,)), ((), ())), preferred_element_type=F32)
        return carry

    lax.fori_loop(0, rows // chunk, finish, 0)
    sketched = sketched_ref[...]
    grams[s] = jnp.dot(sketched.T, sketched, precision=HIGHEST, preferred_element_type=F32)

    def gram_copy(d):
        return remote(grams.at[s], grams.at[s], g_send.at[d], g_recv.at[s], (t, (s + d) % n_s))

    for d in range(1, n_s):
        gram_copy(d).start()
    for d in range(1, n_s):
        owner = (s + d) % n_s
        pltpu.make_async_copy(grams.at[owner], grams.at[owner], g_recv.at[owner]).wait()
    total = grams[0]
    for d in range(1, n_s):
        total = total + grams[d]
    gram_ref[...] = total

    for d in range(1, n_s):
        gram_copy(d).wait_send()
    for d in range(1, n_t):
        packed_copy(d).wait_send()
        half_copy(d).wait_send()
        mate_copy((t + d) % n_t).wait_send()
    for d in range(n_t):
        out_copy((t + d) % n_t).wait()


def basis_kernel(total_rows, gram_ref, sketched_ref, basis_ref, flipped_ref, work, inverse):
    rank = gram_ref.shape[0]
    gram = gram_ref[...]
    row = lax.broadcasted_iota(jnp.int32, (rank, rank), 0)
    col = lax.broadcasted_iota(jnp.int32, (rank, rank), 1)
    eye = row == col
    trace = jnp.sum(jnp.where(eye, gram, 0.0))
    work[...] = gram + jnp.where(eye, SHIFT_SCALE * trace / rank, 0.0)
    inverse[...] = jnp.where(eye, 1.0, 0.0)
    size = 16
    local = lax.broadcasted_iota(jnp.int32, (size, rank), 0)
    for first in range(0, rank, size):
        panel = work[first:first + size, :]
        inv_panel = inverse[first:first + size, :]
        cols = [jnp.broadcast_to(panel[:, first + i:first + i + 1], (size, rank)) for i in range(size)]
        for i in range(size):
            pivot = jnp.broadcast_to(cols[i][i:i + 1, :], (size, rank))
            scale = lax.rsqrt(pivot)
            scale = scale * (1.5 - 0.5 * pivot * scale * scale)
            factor = jnp.where(local > i, cols[i] * scale, 0.0)
            panel_row = panel[i:i + 1, :] * scale
            inv_row = inv_panel[i:i + 1, :] * scale
            panel = jnp.where(local == i, panel_row, panel - factor * panel_row)
            inv_panel = jnp.where(local == i, inv_row, inv_panel - factor * inv_row)
            for j in range(i + 1, size):
                cols[j] = cols[j] - factor * (cols[j][i:i + 1, :] * scale)
        inverse[first:first + size, :] = inv_panel
        rest = first + size
        if rest < rank:
            both = jnp.concatenate([panel, inv_panel], axis=1)
            update = lax.dot_general(
                panel, both, (((0,), (0,)), ((), ())), precision=HIGHEST, preferred_element_type=F32)
            work[rest:, :] -= update[rest:, :rank]
            inverse[rest:, :] -= update[rest:, rank:]
    basis = math.sqrt(total_rows) * lax.dot_general(
        sketched_ref[...], inverse[...], (((1,), (1,)), ((), ())),
        precision=HIGHEST, preferred_element_type=F32)
    basis_ref[...] = basis.astype(BF16)
    flipped_ref[...] = basis.T.astype(BF16)


def project_kernel(
    n_t, n_s, scale, flipped_ref, kernel_in, out_ref,
    kernel_all, partial, to_mate, from_mate, to_far, from_far,
    in_sem, mate_send, mate_recv, far_send, far_recv,
):
    t = lax.axis_index("tgt")
    s = lax.axis_index("src")
    core = s % 2
    y = s // 2
    n_y = n_s // 2
    mate = s + 1 - 2 * core
    per = n_t // n_s
    width = kernel_all.shape[2]

    barrier = pltpu.get_barrier_semaphore()
    pl.semaphore_signal(barrier, inc=1, device_id=(t, mate), device_id_type=MESH)
    for d in range(1, n_y):
        pl.semaphore_signal(barrier, inc=1, device_id=(t, ((y + d) % n_y) * 2 + core), device_id_type=MESH)

    def in_copy(block):
        return pltpu.make_async_copy(kernel_in.at[block], kernel_all.at[block], in_sem.at[block])

    order = [((y + d) % n_y) * 2 + 1 - core for d in range(1, n_y)]
    order += [((y + d) % n_y) * 2 + core for d in range(1, n_y)]
    order += [mate, s]
    for dest in order:
        for piece in range(per):
            in_copy(dest * per + piece).start()
    pl.semaphore_wait(barrier, n_y)

    def product(dest, piece):
        block = dest * per + piece
        in_copy(block).wait()
        return scale * jnp.dot(flipped_ref[...], kernel_all[block], preferred_element_type=F32)

    def mate_copy(d):
        return remote(to_mate.at[d], from_mate.at[d], mate_send.at[d], mate_recv.at[d], (t, mate))

    def far_copy(d):
        return remote(to_far.at[d], from_far.at[d], far_send.at[d], far_recv.at[d],
                      (t, ((y + d) % n_y) * 2 + core))

    def cut(piece):
        return slice(piece * width, (piece + 1) * width)

    for d in range(1, n_y):
        for piece in range(per):
            to_mate[d, :, cut(piece)] = product(order[d - 1], piece).astype(BF16)
        mate_copy(d).start()
    for d in range(1, n_y):
        for piece in range(per):
            partial[d, :, cut(piece)] = product(order[n_y - 2 + d], piece)
    for d in range(1, n_y):
        mate_copy(d).wait_recv()
        to_far[d] = (partial[d] + from_mate[d].astype(F32)).astype(BF16)
        far_copy(d).start()
    for piece in range(per):
        to_mate[0, :, cut(piece)] = product(mate, piece).astype(BF16)
    mate_copy(0).start()
    for piece in range(per):
        partial[0, :, cut(piece)] = product(s, piece)
    mate_copy(0).wait_recv()
    total = partial[0] + from_mate[0].astype(F32)
    for d in range(1, n_y):
        far_copy(d).wait_recv()
        total = total + from_far[d].astype(F32)
    out_ref[...] = total.astype(BF16)
    for d in range(n_y):
        mate_copy(d).wait_send()
    for d in range(1, n_y):
        far_copy(d).wait_send()


def body(target_points, source_points, charges, sketch, far_mask):
    n_t = lax.axis_size("tgt")
    n_s = lax.axis_size("src")
    rows = target_points.shape[2]
    total_rows = rows * n_s
    width = source_points.shape[1]
    rank = sketch.shape[0]
    cluster = width * n_t // far_mask.shape[1]
    vmem = pl.BlockSpec(memory_space=pltpu.VMEM)
    smem = pl.BlockSpec(memory_space=pltpu.SMEM)
    hbm = pl.BlockSpec(memory_space=pl.ANY)
    dma = pltpu.SemaphoreType.DMA
    kernel_all, sketched, gram = pl.pallas_call(
        functools.partial(sketch_kernel, n_t, n_s, cluster),
        out_shape=(
            jax.ShapeDtypeStruct((n_t, rows, width), BF16),
            jax.ShapeDtypeStruct((rows, rank), F32),
            jax.ShapeDtypeStruct((rank, rank), F32),
        ),
        in_specs=[vmem, vmem, vmem, vmem, smem],
        out_specs=(hbm, vmem, vmem),
        scratch_shapes=[
            pltpu.VMEM((n_t, 4, width), F32),
            pltpu.VMEM((n_t, rank, width), BF16),
            pltpu.VMEM((n_t, rows, width), BF16),
            pltpu.VMEM((3, rows, 128), F32),
            pltpu.VMEM((n_s, rank, rank), F32),
            dma((n_t,)), dma((n_t,)), dma((n_t,)), dma((n_t,)), dma((n_t,)), dma((n_t,)),
            dma((n_s,)), dma((n_s,)), dma((n_t,)),
        ],
        compiler_params=pltpu.CompilerParams(
            collective_id=0, has_side_effects=True, vmem_limit_bytes=VMEM_LIMIT),
        name="sketch",
    )(target_points, source_points, charges[None, :], sketch, far_mask)
    basis, flipped = pl.pallas_call(
        functools.partial(basis_kernel, total_rows),
        out_shape=(
            jax.ShapeDtypeStruct((rows, rank), BF16),
            jax.ShapeDtypeStruct((rank, rows), BF16),
        ),
        in_specs=[vmem, vmem],
        out_specs=(vmem, vmem),
        scratch_shapes=[pltpu.VMEM((rank, rank), F32), pltpu.VMEM((rank, rank), F32)],
        name="basis",
    )(gram, sketched)
    n_y = n_s // 2
    span = width * n_t // n_s
    factor = pl.pallas_call(
        functools.partial(project_kernel, n_t, n_s, 1.0 / total_rows),
        out_shape=jax.ShapeDtypeStruct((rank, span), BF16),
        in_specs=[vmem, hbm],
        out_specs=vmem,
        scratch_shapes=[
            pltpu.VMEM((n_t, rows, width), BF16),
            pltpu.VMEM((n_y, rank, span), F32),
            pltpu.VMEM((n_y, rank, span), BF16),
            pltpu.VMEM((n_y, rank, span), BF16),
            pltpu.VMEM((n_y, rank, span), BF16),
            pltpu.VMEM((n_y, rank, span), BF16),
            dma((n_t,)), dma((n_y,)), dma((n_y,)), dma((n_y,)), dma((n_y,)),
        ],
        compiler_params=pltpu.CompilerParams(
            collective_id=1, has_side_effects=True, vmem_limit_bytes=VMEM_LIMIT),
        name="project",
    )(flipped, kernel_all)
    return basis[None], factor[None]


def solution(mesh):
    placed = (P(None, None, "src"), P(None, "tgt"), P("tgt"), P(None, "tgt"), P())
    return jax.shard_map(
        body,
        mesh=mesh,
        in_specs=placed,
        out_specs=(P("tgt", "src", None), P("tgt", None, "src")),
        check_vma=False,
    )
```

```python
import functools
import math

import jax
import jax.numpy as jnp
from jax import lax
from jax.experimental import pallas as pl
from jax.experimental.pallas import tpu as pltpu
from jax.sharding import PartitionSpec as P

SOFTENING = 0.0004
SHIFT_SCALE = 0.05
MESH = pl.DeviceIdType.MESH
HIGHEST = lax.Precision.HIGHEST
F32 = jnp.float32
BF16 = jnp.bfloat16
VMEM_LIMIT = 56 << 20


def remote(src, dst, send_sem, recv_sem, device):
    return pltpu.make_async_remote_copy(
        src_ref=src, dst_ref=dst, send_sem=send_sem, recv_sem=recv_sem,
        device_id=device, device_id_type=MESH,
    )


def sketch_kernel(
    n_t, n_s, cluster, targets_ref, points_ref, charges_ref, sketch_ref, mask_ref,
    kernel_out, sketched_ref, gram_ref,
    packed, columns, kernel_all, target_cols, grams,
    pk_send, pk_recv, sk_send, sk_recv, mate_send, mate_recv, g_send, g_recv, out_sem,
):
    t = lax.axis_index("tgt")
    s = lax.axis_index("src")
    core = s % 2
    mate = s + 1 - 2 * core
    rank, width = sketch_ref.shape
    rows = targets_ref.shape[2]
    half = rank // 2

    barrier = pltpu.get_barrier_semaphore()
    for d in range(1, n_t):
        pl.semaphore_signal(barrier, inc=1, device_id=((t + d) % n_t, s), device_id_type=MESH)
    for d in range(1, n_s):
        pl.semaphore_signal(barrier, inc=1, device_id=(t, (s + d) % n_s), device_id_type=MESH)

    packed[t, 0:3, :] = points_ref[...]
    packed[t, 3:4, :] = charges_ref[...]
    columns[t] = sketch_ref[...]
    pl.semaphore_wait(barrier, n_t + n_s - 2)

    def halves(owner, which):
        return columns.at[owner, pl.ds(pl.multiple_of(which * half, half), half)]

    def packed_copy(d):
        return remote(packed.at[t], packed.at[t], pk_send.at[d], pk_recv.at[t], ((t + d) % n_t, s))

    def half_copy(d):
        return remote(halves(t, core), halves(t, core), sk_send.at[d], sk_recv.at[t], ((t + d) % n_t, s))

    def mate_copy(owner):
        return remote(halves(owner, core), halves(owner, core), mate_send.at[owner], mate_recv.at[owner], (t, mate))

    def out_copy(owner):
        return pltpu.make_async_copy(kernel_all.at[owner], kernel_out.at[owner], out_sem.at[owner])

    for d in range(1, n_t):
        packed_copy(d).start()
    for d in range(1, n_t):
        half_copy(d).start()

    lanes = 128
    stacked = jnp.concatenate(
        [targets_ref[0, pl.ds(t, 1), :], targets_ref[1, pl.ds(t, 1), :], targets_ref[2, pl.ds(t, 1), :],
         jnp.zeros((5, rows), F32)], axis=0)
    for first in range(0, rows, 128):
        block = jnp.concatenate([stacked[:, first:first + 128], jnp.zeros((120, 128), F32)], axis=0).T
        for axis in range(3):
            target_cols[axis, first:first + 128, :] = jnp.broadcast_to(block[:, axis:axis + 1], (128, lanes))
    sketched_ref[...] = jnp.zeros_like(sketched_ref)

    chunk = rows
    sub = 64

    def sweep(owner, previous):
        sx, sy, sz = packed[owner, 0:1, :], packed[owner, 1:2, :], packed[owner, 2:3, :]
        charge = packed[owner, 3:4, :]
        weights = []
        for piece in range(width // lanes):
            near = mask_ref[t, owner * (width // cluster) + piece * lanes // cluster]
            weights.append(charge[:, piece * lanes:(piece + 1) * lanes] * near.astype(F32))

        def step(index, carry):
            base = pl.multiple_of(index * chunk, chunk)
            for inner in range(chunk // sub):
                at = pl.ds(base + inner * sub, sub)
                tx, ty, tz = target_cols[0, at, :], target_cols[1, at, :], target_cols[2, at, :]
                for piece in range(width // lanes):
                    cut = slice(piece * lanes, (piece + 1) * lanes)
                    dx = tx - sx[:, cut]
                    dy = ty - sy[:, cut]
                    dz = tz - sz[:, cut]
                    distance2 = dx * dx + dy * dy + dz * dz + SOFTENING
                    kernel_all[owner, at, cut] = (weights[piece] * lax.rsqrt(distance2)).astype(BF16)
            if previous is not None:
                at = pl.ds(base, chunk)
                sketched_ref[at, :] += lax.dot_general(
                    kernel_all[previous, at, :], columns[previous], (((1,), (1,)), ((), ())),
                    preferred_element_type=F32)
            return carry

        lax.fori_loop(0, rows // chunk, step, 0)

    lag = 2
    ahead = 2

    def at_distance(d):
        return (t + n_t - d) % n_t

    def forward(d):
        owner = at_distance(d)
        pltpu.make_async_copy(halves(owner, core), halves(owner, core), sk_recv.at[owner]).wait()
        mate_copy(owner).start()

    def complete(d):
        owner = at_distance(d)
        pltpu.make_async_copy(halves(owner, 1 - core), halves(owner, 1 - core), mate_recv.at[owner]).wait()

    sweep(t, None)
    out_copy(t).start()

    def visit(d, carry):
        owner = at_distance(d)
        pltpu.make_async_copy(packed.at[owner], packed.at[owner], pk_recv.at[owner]).wait()

        @pl.when(d > lag)
        def _():
            complete(d - lag)

        @pl.when(d >= lag)
        def _():
            sweep(owner, at_distance(d - lag))

        @pl.when(d < lag)
        def _():
            sweep(owner, None)

        out_copy(owner).start()
        for extra in reversed(range(ahead)):
            @pl.when((d * ahead - extra <= ahead * ahead) & (d * ahead - extra < n_t))
            def _():
                forward(d * ahead - extra)

        @pl.when((d > ahead) & (d + ahead < n_t))
        def _():
            forward(d + ahead)

        return carry

    lax.fori_loop(1, n_t, visit, 0)

    def finish(d, carry):
        owner = at_distance(d)
        complete(d)

        def step(index, inner):
            at = pl.ds(pl.multiple_of(index * chunk, chunk), chunk)
            sketched_ref[at, :] += lax.dot_general(
                kernel_all[owner, at, :], columns[owner], (((1,), (1,)), ((), ())), preferred_element_type=F32)
            return inner

        lax.fori_loop(0, rows // chunk, step, 0)
        return carry

    lax.fori_loop(n_t - lag, n_t, finish, 0)
    sketched = sketched_ref[...]
    grams[s] = jnp.dot(sketched.T, sketched, precision=HIGHEST, preferred_element_type=F32)

    def gram_copy(d):
        return remote(grams.at[s], grams.at[s], g_send.at[d], g_recv.at[s], (t, (s + d) % n_s))

    for d in range(1, n_s):
        gram_copy(d).start()
    for d in range(1, n_s):
        owner = (s + d) % n_s
        pltpu.make_async_copy(grams.at[owner], grams.at[owner], g_recv.at[owner]).wait()
    total = grams[0]
    for d in range(1, n_s):
        total = total + grams[d]
    gram_ref[...] = total

    for d in range(1, n_s):
        gram_copy(d).wait_send()
    for d in range(1, n_t):
        packed_copy(d).wait_send()
        half_copy(d).wait_send()
        mate_copy((t + d) % n_t).wait_send()
    for d in range(n_t):
        out_copy((t + d) % n_t).wait()


def basis_kernel(total_rows, gram_ref, sketched_ref, basis_ref, flipped_ref, work, inverse):
    rank = gram_ref.shape[0]
    gram = gram_ref[...]
    row = lax.broadcasted_iota(jnp.int32, (rank, rank), 0)
    col = lax.broadcasted_iota(jnp.int32, (rank, rank), 1)
    eye = row == col
    trace = jnp.sum(jnp.where(eye, gram, 0.0))
    work[...] = gram + jnp.where(eye, SHIFT_SCALE * trace / rank, 0.0)
    inverse[...] = jnp.where(eye, 1.0, 0.0)
    size = 32
    local = lax.broadcasted_iota(jnp.int32, (size, rank), 0)
    for first in range(0, rank, size):
        panel = work[first:first + size, :]
        inv_panel = inverse[first:first + size, :]
        cols = [jnp.broadcast_to(panel[:, first + i:first + i + 1], (size, rank)) for i in range(size)]
        for i in range(size):
            pivot = jnp.broadcast_to(cols[i][i:i + 1, :], (size, rank))
            scale = lax.rsqrt(pivot)
            factor = jnp.where(local > i, cols[i] * scale, 0.0)
            panel_row = panel[i:i + 1, :] * scale
            inv_row = inv_panel[i:i + 1, :] * scale
            panel = jnp.where(local == i, panel_row, panel - factor * panel_row)
            inv_panel = jnp.where(local == i, inv_row, inv_panel - factor * inv_row)
            for j in range(i + 1, size):
                cols[j] = cols[j] - factor * (cols[j][i:i + 1, :] * scale)
        inverse[first:first + size, :] = inv_panel
        rest = first + size
        if rest < rank:
            both = jnp.concatenate([panel, inv_panel], axis=1)
            update = lax.dot_general(
                panel, both, (((0,), (0,)), ((), ())), precision=HIGHEST, preferred_element_type=F32)
            work[rest:, :] -= update[rest:, :rank]
            inverse[rest:, :] -= update[rest:, rank:]
    basis = math.sqrt(total_rows) * lax.dot_general(
        sketched_ref[...], inverse[...], (((1,), (1,)), ((), ())),
        precision=HIGHEST, preferred_element_type=F32)
    basis_ref[...] = basis.astype(BF16)
    flipped_ref[...] = basis.T.astype(BF16)


def project_kernel(
    n_t, n_s, scale, flipped_ref, kernel_in, out_ref,
    kernel_all, partial, to_mate, from_mate, to_far, from_far,
    in_sem, mate_send, mate_recv, far_send, far_recv,
):
    t = lax.axis_index("tgt")
    s = lax.axis_index("src")
    core = s % 2
    y = s // 2
    n_y = n_s // 2
    mate = s + 1 - 2 * core
    per = n_t // n_s
    width = kernel_all.shape[2]

    barrier = pltpu.get_barrier_semaphore()
    pl.semaphore_signal(barrier, inc=1, device_id=(t, mate), device_id_type=MESH)
    for d in range(1, n_y):
        pl.semaphore_signal(barrier, inc=1, device_id=(t, ((y + d) % n_y) * 2 + core), device_id_type=MESH)

    def in_copy(block):
        return pltpu.make_async_copy(kernel_in.at[block], kernel_all.at[block], in_sem.at[block])

    order = [((y + d) % n_y) * 2 + 1 - core for d in range(1, n_y)]
    order += [((y + d) % n_y) * 2 + core for d in range(1, n_y)]
    order += [mate, s]
    for dest in order:
        for piece in range(per):
            in_copy(dest * per + piece).start()
    pl.semaphore_wait(barrier, n_y)

    def product(dest, piece):
        block = dest * per + piece
        in_copy(block).wait()
        return scale * jnp.dot(flipped_ref[...], kernel_all[block], preferred_element_type=F32)

    def mate_copy(d):
        return remote(to_mate.at[d], from_mate.at[d], mate_send.at[d], mate_recv.at[d], (t, mate))

    def far_copy(d):
        return remote(to_far.at[d], from_far.at[d], far_send.at[d], far_recv.at[d],
                      (t, ((y + d) % n_y) * 2 + core))

    def cut(piece):
        return slice(piece * width, (piece + 1) * width)

    for d in range(1, n_y):
        for piece in range(per):
            to_mate[d, :, cut(piece)] = product(order[d - 1], piece).astype(BF16)
        mate_copy(d).start()
    for d in range(1, n_y):
        for piece in range(per):
            partial[d, :, cut(piece)] = product(order[n_y - 2 + d], piece)
    for d in range(1, n_y):
        mate_copy(d).wait_recv()
        to_far[d] = (partial[d] + from_mate[d].astype(F32)).astype(BF16)
        far_copy(d).start()
    for piece in range(per):
        to_mate[0, :, cut(piece)] = product(mate, piece).astype(BF16)
    mate_copy(0).start()
    for piece in range(per):
        partial[0, :, cut(piece)] = product(s, piece)
    mate_copy(0).wait_recv()
    total = partial[0] + from_mate[0].astype(F32)
    for d in range(1, n_y):
        far_copy(d).wait_recv()
        total = total + from_far[d].astype(F32)
    out_ref[...] = total.astype(BF16)
    for d in range(n_y):
        mate_copy(d).wait_send()
    for d in range(1, n_y):
        far_copy(d).wait_send()


def body(target_points, source_points, charges, sketch, far_mask):
    n_t = lax.axis_size("tgt")
    n_s = lax.axis_size("src")
    rows = target_points.shape[2]
    total_rows = rows * n_s
    width = source_points.shape[1]
    rank = sketch.shape[0]
    cluster = width * n_t // far_mask.shape[1]
    vmem = pl.BlockSpec(memory_space=pltpu.VMEM)
    smem = pl.BlockSpec(memory_space=pltpu.SMEM)
    hbm = pl.BlockSpec(memory_space=pl.ANY)
    dma = pltpu.SemaphoreType.DMA
    kernel_all, sketched, gram = pl.pallas_call(
        functools.partial(sketch_kernel, n_t, n_s, cluster),
        out_shape=(
            jax.ShapeDtypeStruct((n_t, rows, width), BF16),
            jax.ShapeDtypeStruct((rows, rank), F32),
            jax.ShapeDtypeStruct((rank, rank), F32),
        ),
        in_specs=[vmem, vmem, vmem, vmem, smem],
        out_specs=(hbm, vmem, vmem),
        scratch_shapes=[
            pltpu.VMEM((n_t, 4, width), F32),
            pltpu.VMEM((n_t, rank, width), BF16),
            pltpu.VMEM((n_t, rows, width), BF16),
            pltpu.VMEM((3, rows, 128), F32),
            pltpu.VMEM((n_s, rank, rank), F32),
            dma((n_t,)), dma((n_t,)), dma((n_t,)), dma((n_t,)), dma((n_t,)), dma((n_t,)),
            dma((n_s,)), dma((n_s,)), dma((n_t,)),
        ],
        compiler_params=pltpu.CompilerParams(
            collective_id=0, has_side_effects=True, vmem_limit_bytes=VMEM_LIMIT),
        name="sketch",
    )(target_points, source_points, charges[None, :], sketch, far_mask)
    basis, flipped = pl.pallas_call(
        functools.partial(basis_kernel, total_rows),
        out_shape=(
            jax.ShapeDtypeStruct((rows, rank), BF16),
            jax.ShapeDtypeStruct((rank, rows), BF16),
        ),
        in_specs=[vmem, vmem],
        out_specs=(vmem, vmem),
        scratch_shapes=[pltpu.VMEM((rank, rank), F32), pltpu.VMEM((rank, rank), F32)],
        name="basis",
    )(gram, sketched)
    n_y = n_s // 2
    span = width * n_t // n_s
    factor = pl.pallas_call(
        functools.partial(project_kernel, n_t, n_s, 1.0 / total_rows),
        out_shape=jax.ShapeDtypeStruct((rank, span), BF16),
        in_specs=[vmem, hbm],
        out_specs=vmem,
        scratch_shapes=[
            pltpu.VMEM((n_t, rows, width), BF16),
            pltpu.VMEM((n_y, rank, span), F32),
            pltpu.VMEM((n_y, rank, span), BF16),
            pltpu.VMEM((n_y, rank, span), BF16),
            pltpu.VMEM((n_y, rank, span), BF16),
            pltpu.VMEM((n_y, rank, span), BF16),
            dma((n_t,)), dma((n_y,)), dma((n_y,)), dma((n_y,)), dma((n_y,)),
        ],
        compiler_params=pltpu.CompilerParams(
            collective_id=1, has_side_effects=True, vmem_limit_bytes=VMEM_LIMIT),
        name="project",
    )(flipped, kernel_all)
    return basis[None], factor[None]


def solution(mesh):
    placed = (P(None, None, "src"), P(None, "tgt"), P("tgt"), P(None, "tgt"), P())
    return jax.shard_map(
        body,
        mesh=mesh,
        in_specs=placed,
        out_specs=(P("tgt", "src", None), P("tgt", None, "src")),
        check_vma=False,
    )
```

```python
import functools
import math

import jax
import jax.numpy as jnp
from jax import lax
from jax.experimental import pallas as pl
from jax.experimental.pallas import tpu as pltpu
from jax.sharding import PartitionSpec as P

SOFTENING = 0.0004
SHIFT_SCALE = 0.05
MESH = pl.DeviceIdType.MESH
HIGHEST = lax.Precision.HIGHEST
F32 = jnp.float32
BF16 = jnp.bfloat16
VMEM_LIMIT = 56 << 20


def remote(src, dst, send_sem, recv_sem, device):
    return pltpu.make_async_remote_copy(
        src_ref=src, dst_ref=dst, send_sem=send_sem, recv_sem=recv_sem,
        device_id=device, device_id_type=MESH,
    )


def sketch_kernel(
    n_t, n_s, cluster, targets_ref, points_ref, charges_ref, sketch_ref, mask_ref,
    kernel_out, sketched_ref, gram_ref,
    packed, columns, kernel_all, target_cols, grams,
    pk_send, pk_recv, sk_send, sk_recv, mate_send, mate_recv, g_send, g_recv, out_sem,
):
    t = lax.axis_index("tgt")
    s = lax.axis_index("src")
    core = s % 2
    mate = s + 1 - 2 * core
    rank, width = sketch_ref.shape
    rows = targets_ref.shape[2]
    half = rank // 2

    barrier = pltpu.get_barrier_semaphore()
    for d in range(1, n_t):
        pl.semaphore_signal(barrier, inc=1, device_id=((t + d) % n_t, s), device_id_type=MESH)
    for d in range(1, n_s):
        pl.semaphore_signal(barrier, inc=1, device_id=(t, (s + d) % n_s), device_id_type=MESH)

    packed[t, 0:3, :] = points_ref[...]
    packed[t, 3:4, :] = charges_ref[...]
    columns[t] = sketch_ref[...]
    pl.semaphore_wait(barrier, n_t + n_s - 2)

    def halves(owner, which):
        return columns.at[owner, pl.ds(pl.multiple_of(which * half, half), half)]

    def packed_copy(d):
        return remote(packed.at[t], packed.at[t], pk_send.at[d], pk_recv.at[t], ((t + d) % n_t, s))

    def half_copy(d):
        return remote(halves(t, core), halves(t, core), sk_send.at[d], sk_recv.at[t], ((t + d) % n_t, s))

    def mate_copy(owner):
        return remote(halves(owner, core), halves(owner, core), mate_send.at[owner], mate_recv.at[owner], (t, mate))

    def out_copy(owner):
        return pltpu.make_async_copy(kernel_all.at[owner], kernel_out.at[owner], out_sem.at[owner])

    for d in range(1, n_t):
        packed_copy(d).start()
    for d in range(1, n_t):
        half_copy(d).start()

    def parts(values):
        first = values.astype(BF16).astype(F32)
        second = (values - first).astype(BF16).astype(F32)
        return first, second, values - first - second

    lanes = 128
    tx = targets_ref[0, pl.ds(t, 1), :] - 0.5
    ty = targets_ref[1, pl.ds(t, 1), :] - 0.5
    tz = targets_ref[2, pl.ds(t, 1), :] - 0.5
    t1, t2, t3 = parts(jnp.concatenate(
        [tx, ty, tz, jnp.ones_like(tx), tx * tx + ty * ty + tz * tz, jnp.zeros((3, rows), F32)], axis=0))
    stacked = jnp.concatenate([t1, t1, t2, t2, t1, t3, jnp.zeros((80, rows), F32)], axis=0)
    for first in range(0, rows, 128):
        target_cols[first:first + 128, :] = stacked[:, first:first + 128].T.astype(BF16)
    sketched_ref[...] = jnp.zeros_like(sketched_ref)

    chunk = rows
    sub = 128

    def sweep(owner, previous):
        sx, sy, sz = packed[owner, 0:1, :] - 0.5, packed[owner, 1:2, :] - 0.5, packed[owner, 2:3, :] - 0.5
        charge = packed[owner, 3:4, :]
        s1, s2, s3 = parts(jnp.concatenate(
            [-2.0 * sx, -2.0 * sy, -2.0 * sz, sx * sx + sy * sy + sz * sz + SOFTENING,
             jnp.ones_like(sx), jnp.zeros((3, width), F32)], axis=0))
        features = jnp.concatenate(
            [s1, s2, s1, s2, s3, s1, jnp.zeros((80, width), F32)], axis=0).astype(BF16)
        weights = []
        for piece in range(width // lanes):
            near = mask_ref[t, owner * (width // cluster) + piece * lanes // cluster]
            weights.append(charge[:, piece * lanes:(piece + 1) * lanes] * near.astype(F32))

        def step(index, carry):
            base = pl.multiple_of(index * chunk, chunk)
            for inner in range(chunk // sub):
                at = pl.ds(base + inner * sub, sub)
                distance2 = jnp.dot(target_cols[at, :], features, preferred_element_type=F32)
                for piece in range(width // lanes):
                    cut = slice(piece * lanes, (piece + 1) * lanes)
                    kernel_all[owner, at, cut] = (weights[piece] * lax.rsqrt(distance2[:, cut])).astype(BF16)
            if previous is not None:
                at = pl.ds(base, chunk)
                sketched_ref[at, :] += lax.dot_general(
                    kernel_all[previous, at, :], columns[previous], (((1,), (1,)), ((), ())),
                    preferred_element_type=F32)
            return carry

        lax.fori_loop(0, rows // chunk, step, 0)

    lag = 2
    ahead = 2

    def at_distance(d):
        return (t + n_t - d) % n_t

    def forward(d):
        owner = at_distance(d)
        pltpu.make_async_copy(halves(owner, core), halves(owner, core), sk_recv.at[owner]).wait()
        mate_copy(owner).start()

    def complete(d):
        owner = at_distance(d)
        pltpu.make_async_copy(halves(owner, 1 - core), halves(owner, 1 - core), mate_recv.at[owner]).wait()

    sweep(t, None)
    out_copy(t).start()

    def visit(d, carry):
        owner = at_distance(d)
        pltpu.make_async_copy(packed.at[owner], packed.at[owner], pk_recv.at[owner]).wait()

        @pl.when(d > lag)
        def _():
            complete(d - lag)

        @pl.when(d >= lag)
        def _():
            sweep(owner, at_distance(d - lag))

        @pl.when(d < lag)
        def _():
            sweep(owner, None)

        out_copy(owner).start()
        for extra in reversed(range(ahead)):
            @pl.when((d * ahead - extra <= ahead * ahead) & (d * ahead - extra < n_t))
            def _():
                forward(d * ahead - extra)

        @pl.when((d > ahead) & (d + ahead < n_t))
        def _():
            forward(d + ahead)

        return carry

    lax.fori_loop(1, n_t, visit, 0)

    def finish(d, carry):
        owner = at_distance(d)
        complete(d)

        def step(index, inner):
            at = pl.ds(pl.multiple_of(index * chunk, chunk), chunk)
            sketched_ref[at, :] += lax.dot_general(
                kernel_all[owner, at, :], columns[owner], (((1,), (1,)), ((), ())), preferred_element_type=F32)
            return inner

        lax.fori_loop(0, rows // chunk, step, 0)
        return carry

    lax.fori_loop(n_t - lag, n_t, finish, 0)
    sketched = sketched_ref[...]
    grams[s] = jnp.dot(sketched.T, sketched, precision=HIGHEST, preferred_element_type=F32)

    def gram_copy(d):
        return remote(grams.at[s], grams.at[s], g_send.at[d], g_recv.at[s], (t, (s + d) % n_s))

    for d in range(1, n_s):
        gram_copy(d).start()
    for d in range(1, n_s):
        owner = (s + d) % n_s
        pltpu.make_async_copy(grams.at[owner], grams.at[owner], g_recv.at[owner]).wait()
    total = grams[0]
    for d in range(1, n_s):
        total = total + grams[d]
    gram_ref[...] = total

    for d in range(1, n_s):
        gram_copy(d).wait_send()
    for d in range(1, n_t):
        packed_copy(d).wait_send()
        half_copy(d).wait_send()
        mate_copy((t + d) % n_t).wait_send()
    for d in range(n_t):
        out_copy((t + d) % n_t).wait()


def basis_kernel(total_rows, gram_ref, sketched_ref, basis_ref, flipped_ref, work, inverse):
    rank = gram_ref.shape[0]
    gram = gram_ref[...]
    row = lax.broadcasted_iota(jnp.int32, (rank, rank), 0)
    col = lax.broadcasted_iota(jnp.int32, (rank, rank), 1)
    eye = row == col
    trace = jnp.sum(jnp.where(eye, gram, 0.0))
    work[...] = gram + jnp.where(eye, SHIFT_SCALE * trace / rank, 0.0)
    inverse[...] = jnp.where(eye, 1.0, 0.0)
    size = 32
    local = lax.broadcasted_iota(jnp.int32, (size, rank), 0)
    for first in range(0, rank, size):
        panel = work[first:first + size, :]
        inv_panel = inverse[first:first + size, :]
        cols = [jnp.broadcast_to(panel[:, first + i:first + i + 1], (size, rank)) for i in range(size)]
        for i in range(size):
            pivot = jnp.broadcast_to(cols[i][i:i + 1, :], (size, rank))
            scale = lax.rsqrt(pivot)
            factor = jnp.where(local > i, cols[i] * scale, 0.0)
            panel_row = panel[i:i + 1, :] * scale
            inv_row = inv_panel[i:i + 1, :] * scale
            panel = jnp.where(local == i, panel_row, panel - factor * panel_row)
            inv_panel = jnp.where(local == i, inv_row, inv_panel - factor * inv_row)
            for j in range(i + 1, size):
                cols[j] = cols[j] - factor * (cols[j][i:i + 1, :] * scale)
        inverse[first:first + size, :] = inv_panel
        rest = first + size
        if rest < rank:
            both = jnp.concatenate([panel, inv_panel], axis=1)
            update = lax.dot_general(
                panel, both, (((0,), (0,)), ((), ())), precision=HIGHEST, preferred_element_type=F32)
            work[rest:, :] -= update[rest:, :rank]
            inverse[rest:, :] -= update[rest:, rank:]
    basis = math.sqrt(total_rows) * lax.dot_general(
        sketched_ref[...], inverse[...], (((1,), (1,)), ((), ())),
        precision=HIGHEST, preferred_element_type=F32)
    basis_ref[...] = basis.astype(BF16)
    flipped_ref[...] = basis.T.astype(BF16)


def project_kernel(
    n_t, n_s, scale, flipped_ref, kernel_in, out_ref,
    kernel_all, partial, to_mate, from_mate, to_far, from_far,
    in_sem, mate_send, mate_recv, far_send, far_recv,
):
    t = lax.axis_index("tgt")
    s = lax.axis_index("src")
    core = s % 2
    y = s // 2
    n_y = n_s // 2
    mate = s + 1 - 2 * core
    per = n_t // n_s
    width = kernel_all.shape[2]

    barrier = pltpu.get_barrier_semaphore()
    pl.semaphore_signal(barrier, inc=1, device_id=(t, mate), device_id_type=MESH)
    for d in range(1, n_y):
        pl.semaphore_signal(barrier, inc=1, device_id=(t, ((y + d) % n_y) * 2 + core), device_id_type=MESH)

    def in_copy(block):
        return pltpu.make_async_copy(kernel_in.at[block], kernel_all.at[block], in_sem.at[block])

    order = [((y + d) % n_y) * 2 + 1 - core for d in range(1, n_y)]
    order += [((y + d) % n_y) * 2 + core for d in range(1, n_y)]
    order += [mate, s]
    for dest in order:
        for piece in range(per):
            in_copy(dest * per + piece).start()
    pl.semaphore_wait(barrier, n_y)

    def product(dest, piece):
        block = dest * per + piece
        in_copy(block).wait()
        return scale * jnp.dot(flipped_ref[...], kernel_all[block], preferred_element_type=F32)

    def mate_copy(d):
        return remote(to_mate.at[d], from_mate.at[d], mate_send.at[d], mate_recv.at[d], (t, mate))

    def far_copy(d):
        return remote(to_far.at[d], from_far.at[d], far_send.at[d], far_recv.at[d],
                      (t, ((y + d) % n_y) * 2 + core))

    def cut(piece):
        return slice(piece * width, (piece + 1) * width)

    for d in range(1, n_y):
        for piece in range(per):
            to_mate[d, :, cut(piece)] = product(order[d - 1], piece).astype(BF16)
        mate_copy(d).start()
    for d in range(1, n_y):
        for piece in range(per):
            partial[d, :, cut(piece)] = product(order[n_y - 2 + d], piece)
    for d in range(1, n_y):
        mate_copy(d).wait_recv()
        to_far[d] = (partial[d] + from_mate[d].astype(F32)).astype(BF16)
        far_copy(d).start()
    for piece in range(per):
        to_mate[0, :, cut(piece)] = product(mate, piece).astype(BF16)
    mate_copy(0).start()
    for piece in range(per):
        partial[0, :, cut(piece)] = product(s, piece)
    mate_copy(0).wait_recv()
    total = partial[0] + from_mate[0].astype(F32)
    for d in range(1, n_y):
        far_copy(d).wait_recv()
        total = total + from_far[d].astype(F32)
    out_ref[...] = total.astype(BF16)
    for d in range(n_y):
        mate_copy(d).wait_send()
    for d in range(1, n_y):
        far_copy(d).wait_send()


def body(target_points, source_points, charges, sketch, far_mask):
    n_t = lax.axis_size("tgt")
    n_s = lax.axis_size("src")
    rows = target_points.shape[2]
    total_rows = rows * n_s
    width = source_points.shape[1]
    rank = sketch.shape[0]
    cluster = width * n_t // far_mask.shape[1]
    vmem = pl.BlockSpec(memory_space=pltpu.VMEM)
    smem = pl.BlockSpec(memory_space=pltpu.SMEM)
    hbm = pl.BlockSpec(memory_space=pl.ANY)
    dma = pltpu.SemaphoreType.DMA
    kernel_all, sketched, gram = pl.pallas_call(
        functools.partial(sketch_kernel, n_t, n_s, cluster),
        out_shape=(
            jax.ShapeDtypeStruct((n_t, rows, width), BF16),
            jax.ShapeDtypeStruct((rows, rank), F32),
            jax.ShapeDtypeStruct((rank, rank), F32),
        ),
        in_specs=[vmem, vmem, vmem, vmem, smem],
        out_specs=(hbm, vmem, vmem),
        scratch_shapes=[
            pltpu.VMEM((n_t, 4, width), F32),
            pltpu.VMEM((n_t, rank, width), BF16),
            pltpu.VMEM((n_t, rows, width), BF16),
            pltpu.VMEM((rows, 128), BF16),
            pltpu.VMEM((n_s, rank, rank), F32),
            dma((n_t,)), dma((n_t,)), dma((n_t,)), dma((n_t,)), dma((n_t,)), dma((n_t,)),
            dma((n_s,)), dma((n_s,)), dma((n_t,)),
        ],
        compiler_params=pltpu.CompilerParams(
            collective_id=0, has_side_effects=True, vmem_limit_bytes=VMEM_LIMIT),
        name="sketch",
    )(target_points, source_points, charges[None, :], sketch, far_mask)
    basis, flipped = pl.pallas_call(
        functools.partial(basis_kernel, total_rows),
        out_shape=(
            jax.ShapeDtypeStruct((rows, rank), BF16),
            jax.ShapeDtypeStruct((rank, rows), BF16),
        ),
        in_specs=[vmem, vmem],
        out_specs=(vmem, vmem),
        scratch_shapes=[pltpu.VMEM((rank, rank), F32), pltpu.VMEM((rank, rank), F32)],
        name="basis",
    )(gram, sketched)
    n_y = n_s // 2
    span = width * n_t // n_s
    factor = pl.pallas_call(
        functools.partial(project_kernel, n_t, n_s, 1.0 / total_rows),
        out_shape=jax.ShapeDtypeStruct((rank, span), BF16),
        in_specs=[vmem, hbm],
        out_specs=vmem,
        scratch_shapes=[
            pltpu.VMEM((n_t, rows, width), BF16),
            pltpu.VMEM((n_y, rank, span), F32),
            pltpu.VMEM((n_y, rank, span), BF16),
            pltpu.VMEM((n_y, rank, span), BF16),
            pltpu.VMEM((n_y, rank, span), BF16),
            pltpu.VMEM((n_y, rank, span), BF16),
            dma((n_t,)), dma((n_y,)), dma((n_y,)), dma((n_y,)), dma((n_y,)),
        ],
        compiler_params=pltpu.CompilerParams(
            collective_id=1, has_side_effects=True, vmem_limit_bytes=VMEM_LIMIT),
        name="project",
    )(flipped, kernel_all)
    return basis[None], factor[None]


def solution(mesh):
    placed = (P(None, None, "src"), P(None, "tgt"), P("tgt"), P(None, "tgt"), P())
    return jax.shard_map(
        body,
        mesh=mesh,
        in_specs=placed,
        out_specs=(P("tgt", "src", None), P("tgt", None, "src")),
        check_vma=False,
    )
```
